32 devices in a mesh: grp: 4 (over y, x), col: 8 (over z, core).
Axes of the slice: x: 2, y: 2, z: 4, core: 2. Of those that a mesh axis runs over, the one named last changes fastest.
Arguments:
- embeddings: bfloat16 [4096, 1024], P(('grp', 'col')), may hold values from -80 to 80
- labels: int32 [4096, 1], P(('grp', 'col')), may hold values from 0 to 7; in each aligned block of 128 rows (0 to 127, 128 to 255, ...) at most 38 rows name the same one
- row_order: int32 [4096], P(('grp', 'col')), may hold values from 0 to 4095, each once
Outputs:
- nearest: float32 [4096], P(('grp', 'col'))
The draws below stay inside these ranges and needn't reach their ends.
Inputs may be any that keep to these rules, and one draw needn't show every extreme that they name: `labels`: each aligned block of 128 rows (the rows of one device) holds at most 38 rows of any one cluster.
All inputs are finite; a program needn't handle non-finite values.
Results may differ from the reference program's by a relative error of at most 0.0005.
Values may be sent and summed in bfloat16 or wider, within the bound.
No kernel may reach another device: no remote copies, remote signals or barrier semaphores. Data moves between devices by JAX's collectives and lax.ppermute only.
A program may use at most 192 MiB of HBM per device.

```python
import math
import jax
import jax.numpy as jnp
import numpy as np
from jax import lax

E = 1024
R_DEV = 128
CLUSTERS = 8
MOST = 38
ROWS = 4096
N_GRP = 4
N_COL = 8


def draw_embeddings(key, part):
    key_topic, key_center, key_noise = jax.random.split(key, 3)
    topic = jax.random.randint(key_topic, (ROWS,), 0, 512)
    centers = jax.random.normal(key_center, (512, E), jnp.float32)
    picked = jnp.take(centers, topic, axis=0)
    noise = jax.random.normal(key_noise, (ROWS, E), jnp.float32)
    return jnp.clip(picked + noise, -80.0, 80.0).astype(jnp.bfloat16)


def assign_block(key, own, number, rows, count, top, most, slope):
    ranking = jax.random.permutation(key, count)
    heavy_load, usual = portions_of(count, rows * top, most, slope, True), portions_of(count, rows * top, most, slope, False)
    places = jnp.arange(count)

    def named(lengths, offset_by):
        used = int((lengths > 0).sum())
        fixed = max(1, used // 4)
        passed = fixed + (places - fixed + offset_by * (used - fixed)) % max(1, count - fixed)
        return jnp.zeros((count,), jnp.int32).at[ranking[jnp.where(places < fixed, places, passed)]].set(jnp.asarray(lengths, jnp.int32))

    lengths = jnp.where(number % 4 == 0, named(heavy_load, number // 4), named(usual, number - number // 4 - 1))
    mixed = jax.random.permutation(jax.random.fold_in(own, 3), count)
    donor, taker = mixed[0:count // 2 * 2:2], mixed[1:count // 2 * 2:2]
    margin = jnp.minimum(lengths[donor] - 1, most - lengths[taker]) // 2
    margin = jnp.where((donor == ranking[0]) | (taker == ranking[0]) | (lengths[taker] == 0), 0, jnp.maximum(margin, 0))
    passed = jax.random.randint(jax.random.fold_in(own, 4), (count // 2,), 0, 1 << 20) % (margin + 1)
    lengths = lengths.at[donor].add(-passed).at[taker].add(passed)
    items = jnp.searchsorted(jnp.cumsum(lengths), jnp.arange(rows * top), side="right").astype(jnp.int32)
    listing = items.reshape(top, rows).T
    listing = listing[jax.random.permutation(jax.random.fold_in(own, 1), rows)]
    offset_by = jax.random.randint(jax.random.fold_in(own, 2), (rows, 1), 0, top)
    return jnp.take_along_axis(listing, (jnp.arange(top)[None, :] + offset_by) % top, axis=1)


def portions_of(amount, total, reach, slope, full):
    portions = [(1 << 20) // math.isqrt(grade ** slope) + 1 for grade in range(1, amount + 1)]
    largest = reach if full else min(reach, max(-(-total // amount), total * portions[0] // sum(portions)))
    least = 1 if total - largest >= amount - 1 else 0
    given, surplus = [largest] + [least] * (amount - 1), total - largest - least * (amount - 1)
    while surplus > 0:
        free = [i for i in range(1, amount) if given[i] < largest] or [i for i in range(1, amount) if given[i] < reach]
        pool, remaining = sum([portions[i] for i in free]), surplus
        for i in free:
            more = min(reach - given[i], max(1, remaining * portions[i] // pool), surplus)
            given[i] = given[i] + more
            surplus = surplus - more
    return np.array(given)


def setup_inputs(seed: int = 0) -> dict:
    arg_keys = jax.random.split(jax.random.key(seed), 4)
    embeddings = draw_embeddings(jax.random.fold_in(arg_keys[3], 71), 0)
    labels_keys = jax.random.split(jax.random.fold_in(arg_keys[1], 1), ROWS // R_DEV)
    labels_turns = jax.random.permutation(jax.random.fold_in(arg_keys[1], 3), ROWS // R_DEV)
    labels = jax.vmap(lambda own, number: assign_block(jax.random.fold_in(arg_keys[1], 2), own, number, R_DEV, CLUSTERS, 1, MOST, 2))(labels_keys, labels_turns).reshape((ROWS, 1))
    row_order = jax.random.permutation(arg_keys[2], ROWS).astype(jnp.int32)
    return dict(embeddings=embeddings, labels=labels, row_order=row_order)


def reference(embeddings, labels, row_order):
    values = embeddings.astype(jnp.float32)
    unit = (values / jnp.sqrt(lax.optimization_barrier(jnp.sum(values * values, axis=1, keepdims=True)) + 1e-06)).astype(jnp.bfloat16)
    cluster_of = labels[:, 0].astype(jnp.int32)
    sort_key = cluster_of * ROWS + row_order
    sort_order = jnp.argsort(sort_key, stable=True).astype(jnp.int32)
    sorted_emb = jnp.take(unit, sort_order, axis=0).astype(jnp.float32)
    sorted_cls = jnp.take(cluster_of, sort_order, axis=0)
    sorted_pos = jnp.take(row_order, sort_order, axis=0)
    window = N_GRP * N_COL * MOST
    block_rows = 512
    pad_emb = jnp.concatenate([jnp.zeros((window, E), jnp.float32), sorted_emb], 0)
    pad_cls = jnp.concatenate([jnp.full((window,), -1, jnp.int32), sorted_cls], 0)
    pad_pos = jnp.concatenate([jnp.full((window,), ROWS, jnp.int32), sorted_pos], 0)

    def one_block(start):
        queries = lax.dynamic_slice_in_dim(sorted_emb, start, block_rows, 0)
        query_cls = lax.dynamic_slice_in_dim(sorted_cls, start, block_rows, 0)
        query_pos = lax.dynamic_slice_in_dim(sorted_pos, start, block_rows, 0)
        keys_emb = lax.dynamic_slice_in_dim(pad_emb, start, window + block_rows, 0)
        keys_cls = lax.dynamic_slice_in_dim(pad_cls, start, window + block_rows, 0)
        keys_pos = lax.dynamic_slice_in_dim(pad_pos, start, window + block_rows, 0)
        scores = lax.dot_general(queries, keys_emb, (((1,), (1,)), ((), ())), precision=lax.Precision.HIGHEST, preferred_element_type=jnp.float32)
        allowed = (keys_cls[None, :] == query_cls[:, None]) & (keys_pos[None, :] < query_pos[:, None])
        return lax.optimization_barrier(jnp.max(jnp.where(allowed, scores, jnp.float32(-1.0)), axis=1))
    starts = jnp.arange(ROWS // block_rows, dtype=jnp.int32) * block_rows
    best_sim = lax.map(one_block, starts).reshape(ROWS)
    return jnp.zeros((ROWS,), jnp.float32).at[sort_order].set(best_sim)
```

```python
import functools

import jax
import jax.numpy as jnp
from jax import lax
from jax.experimental import pallas as pl
from jax.experimental.pallas import tpu as pltpu
from jax.sharding import PartitionSpec as P


AXES = ("grp", "col")
EPSILON = 1e-06
CORES = 2
META = 8
BASE = 256.0


def prepare_kernel(emb_ref, labels_ref, order_ref, block_ref):
    rows, width = emb_ref.shape
    values = emb_ref[...].astype(jnp.float32)
    total = jnp.sum(values * values, axis=1, keepdims=True)
    block_ref[:rows, :] = (values * (1.0 / jnp.sqrt(total + EPSILON))).astype(jnp.bfloat16)
    order = order_ref[...]
    which = lax.broadcasted_iota(jnp.int32, (META, rows), 0)
    meta = jnp.where(
        which == 0, order >> 8, jnp.where(which == 1, order & 255, jnp.where(which == 2, labels_ref[...], 0))
    )
    block_ref[rows:, :] = jnp.zeros((META, width), jnp.bfloat16)
    block_ref[rows:, :rows] = meta.astype(jnp.float32).astype(jnp.bfloat16)


def prepare(embeddings, labels, row_order):
    rows, width = embeddings.shape
    return pl.pallas_call(
        prepare_kernel,
        out_shape=jax.ShapeDtypeStruct((rows + META, width), jnp.bfloat16),
        in_specs=[pl.BlockSpec(memory_space=pltpu.VMEM)] * 3,
        out_specs=pl.BlockSpec(memory_space=pltpu.VMEM),
    )(embeddings, labels.reshape(1, rows), row_order.reshape(1, rows))


def keys_of(block_ref, rows):
    meta = block_ref[rows:, :rows].astype(jnp.float32)
    base = meta[2:3, :] * (BASE * BASE)
    return base, base + meta[0:1, :] * BASE + meta[1:2, :]


def compare_kernel(n_queries, n_keys, *refs):
    query_refs, key_refs, out_ref = refs[:n_queries], refs[n_queries : n_queries + n_keys], refs[-1]
    rows = out_ref.shape[1]
    best = [jnp.full((8, rows), -1.0, jnp.float32) for _ in query_refs]
    bounds = [keys_of(ref, rows) for ref in query_refs]
    for key_ref in key_refs:
        _, key = keys_of(key_ref, rows)
        key = jnp.broadcast_to(key, (rows, rows)).T
        for i, query_ref in enumerate(query_refs):
            scores = lax.dot_general(
                key_ref[:rows, :], query_ref[:rows, :], (((1,), (1,)), ((), ())), preferred_element_type=jnp.float32
            )
            first, own = bounds[i]
            earlier = (key >= first) & (key < own)
            scores = jnp.where(earlier, scores, -1.0)
            best[i] = jnp.maximum(best[i], jnp.max(scores.reshape(rows // 8, 8, rows), axis=0))
    for i in range(n_queries):
        out_ref[i : i + 1, :] = jnp.max(best[i], axis=0, keepdims=True)


def compare(queries, keys):
    rows = queries[0].shape[0] - META
    return pl.pallas_call(
        functools.partial(compare_kernel, len(queries), len(keys)),
        out_shape=jax.ShapeDtypeStruct((len(queries), rows), jnp.float32),
        in_specs=[pl.BlockSpec(memory_space=pltpu.VMEM)] * (len(queries) + len(keys)),
        out_specs=pl.BlockSpec(memory_space=pltpu.VMEM),
        cost_estimate=pl.CostEstimate(
            flops=2 * len(queries) * len(keys) * rows * rows * queries[0].shape[1],
            bytes_accessed=(len(queries) + len(keys)) * queries[0].size * 2,
            transcendentals=0,
        ),
    )(*queries, *keys)


class Grid:
    def __init__(self, n_grp, n_col):
        places = n_col // CORES
        near = 2
        while near * near * 2 <= places:
            near *= 2
        self.sizes = dict(outer=n_grp // 2, inner=2, far=places // near, near=near, core=CORES)

    def shift(self, **by):
        names, sizes = list(self.sizes), list(self.sizes.values())
        pairs = []
        for source in range(functools.reduce(lambda a, b: a * b, sizes)):
            rest, at = source, {}
            for name, size in zip(reversed(names), reversed(sizes)):
                rest, at[name] = divmod(rest, size)
            target = 0
            for name, size in zip(names, sizes):
                target = target * size + (at[name] + by.get(name, 0)) % size
            pairs.append((source, target))
        return pairs

    def send(self, x, **by):
        return lax.ppermute(x, AXES, self.shift(**by))


def on_device(embeddings, labels, row_order):
    grid = Grid(lax.axis_size("grp"), lax.axis_size("col"))
    size = grid.sizes
    block = prepare(embeddings, labels, row_order)
    far = [block] + [grid.send(block, far=i) for i in range(1, size["far"])]
    near = [block] + [grid.send(block, near=i) for i in range(1, size["near"])]
    keys = list(far)
    for i in range(1, size["outer"]):
        keys += [grid.send(b, outer=i) for b in far]
    queries = {(0, j): b for j, b in enumerate(near)}
    for i in range(1, size["inner"]):
        queries.update({(i, j): grid.send(b, inner=i) for j, b in enumerate(near)})
    keys += [grid.send(b, core=1) for b in keys]
    places = list(queries)
    partial = compare([queries[p] for p in places], keys)
    best = partial[0]
    for row, (i, j) in enumerate(places):
        if row:
            best = jnp.maximum(best, grid.send(partial[row], inner=-i, near=-j))
    return best


def solution(mesh):
    in_specs = (P(AXES, None), P(AXES, None), P(AXES))
    return jax.shard_map(on_device, mesh=mesh, in_specs=in_specs, out_specs=P(AXES), check_vma=False)
```
